256 devices in a mesh: dp: 64 (over z, y, core), tensor: 4 (over x).
Axes of the slice: x: 4, y: 4, z: 8, core: 2. Of those that a mesh axis runs over, the one named last changes fastest.
Arguments:
- hidden_in: bfloat16 [2048, 4096], P('dp'), may hold values from -6 to 6
- norm_gain: float32 [4096], replicated, may hold values from 0.5 to 1.5
- w_in: bfloat16 [4096, 2, 4, 2048], P(None, None, 'tensor', 'dp'), may hold values from -0.09375 to 0.09375
- conv_w: float32 [4, 8192], P(None, 'tensor'), may hold values from -3 to 3
- conv_b: float32 [8192], P('tensor'), may hold values from -2 to 2
- w_dt_low: bfloat16 [8192, 256], P('tensor'), may hold values from -0.0625 to 0.0625
- w_bc: bfloat16 [32, 8192], P(None, 'tensor'), may hold values from -0.0625 to 0.0625
- w_dt: bfloat16 [256, 8192], P(None, 'tensor'), may hold values from -0.375 to 0.375
- dt_bias: float32 [8192], P('tensor'), may hold values from -5 to -1.5
- a_log: float32 [16, 8192], P(None, 'tensor'), may hold values from 0 to 2.77
- d_skip: float32 [8192], P('tensor'), may hold values from 0.5 to 1.5
- w_out: bfloat16 [8192, 4096], P('tensor', 'dp'), may hold values from -0.0625 to 0.0625
- conv_state: bfloat16 [2048, 3, 8192], P('dp', None, 'tensor'), may hold values from -6 to 6
- ssm_state: float32 [2048, 16, 8192], P('dp', None, 'tensor'), may hold values from -6 to 6
- lengths: int32 [2048], P('dp'), may hold values from 0 to 5
- active_ids: int32 [64, 32], P('dp'), may hold values from 0 to 31, each once within a row
- active_count: int32 [64], P('dp'), may hold values from 1 to 24, as said below
Outputs:
- mixed: bfloat16 [2048, 4096], P('dp', 'tensor')
- conv_next: bfloat16 [2048, 3, 8192], P('dp', None, 'tensor')
- ssm_next: float32 [2048, 16, 8192], P('dp', None, 'tensor')
The draws below stay inside these ranges and needn't reach their ends.
Inputs may be any that keep to these rules, and one draw needn't show every extreme that they name: `active_count`: at most 24 slots of a dp index are active; some dp index has exactly 24. `active_ids`: each row lists every slot 0 to 31 of its dp index once.
All inputs are finite; a program needn't handle non-finite values.
Results may differ from the reference program's by a relative error of at most 0.014.
Values may be sent and summed in bfloat16 or wider, within the bound.
A program may use at most 128 MiB of HBM per device.

```python
import jax
import jax.numpy as jnp
from jax import lax

D = 4096
E = 8192
N = 16
R = 256
K = 4
SEQ_DEV = 32
ACT_MAX = 24
BATCH = 2048
N_DP = 64
N_TENSOR = 4


def draw_active_count(key, part):
    first, second, third = jax.random.split(jax.random.fold_in(key, 17), 3)
    one_draw = jax.random.randint(first, (N_DP,), 1, ACT_MAX + 1)
    two_draw = jax.random.randint(second, (N_DP,), 1, ACT_MAX + 1)
    skewed = jnp.minimum(one_draw, two_draw)
    chosen = jax.random.randint(third, (), 0, N_DP)
    return skewed.at[chosen].set(ACT_MAX).astype(jnp.int32)


def set_ends(entries, stream_key, least, top_value):
    shape = entries.shape
    index_at = [jax.random.randint(jax.random.fold_in(stream_key, axis), (), 0, shape[axis]) for axis in range(len(shape))]
    entries = entries.at[tuple(index_at)].set(least)
    longest = shape.index(max(shape))
    index_at[longest] = (index_at[longest] + 1) % shape[longest]
    return entries.at[tuple(index_at)].set(top_value)


def levels(rng, extent, cuts, low, largest):
    factor_of = 1.0
    for dim, shards_of in cuts:
        draws = jax.random.uniform(jax.random.fold_in(jax.random.fold_in(rng, 6), dim), (shards_of,), jnp.float32, low / len(cuts), largest / len(cuts))
        factor_of = factor_of * jnp.repeat(jnp.exp(draws), extent[dim] // shards_of).reshape((-1,) + (1,) * (len(extent) - 1 - dim))
    return factor_of


def scatter_about(own_key, shape, width, bound, cuts=(), kind=jnp.bfloat16):
    values = jax.random.normal(own_key, shape, jnp.float32) * width
    if len(cuts) > 0:
        values = levels(own_key, shape, cuts, -0.22, 0.18) * values
    return jnp.clip(values, min=-bound, max=bound).astype(kind)


def setup_inputs(seed: int = 0) -> dict:
    arg_keys = jax.random.split(jax.random.key(seed), 18)
    hidden_in = scatter_about(arg_keys[0], (BATCH, D), 1.0, 6.0, ((0, 64),))
    norm_gain = jnp.clip(1.0 + 0.1 * jax.random.normal(arg_keys[1], (D,), jnp.float32), 0.5, 1.5)
    w_in = scatter_about(arg_keys[2], (D, 2, N_TENSOR, E // N_TENSOR), D ** -0.5, 0.09375, ((2, 4), (3, 64)))
    conv_w = scatter_about(arg_keys[3], (K, E), 0.5, 3.0, ((1, 4),), jnp.float32)
    conv_b = scatter_about(arg_keys[4], (E,), 0.3, 2.0, ((0, 4),), jnp.float32)
    w_dt_low = scatter_about(arg_keys[5], (E, R), E ** -0.5, 0.0625, ((0, 4),))
    w_bc = scatter_about(arg_keys[6], (2 * N, E), E ** -0.5, 0.0625, ((1, 4),))
    w_dt = scatter_about(arg_keys[7], (R, E), R ** -0.5, 0.375, ((1, 4),))
    dt_bias = jnp.clip(-5.0 + 3.5 * jax.random.uniform(arg_keys[8], (E,), jnp.float32) ** levels(arg_keys[8], (E,), ((0, 4),), -0.2, 0.2), -5.0, -1.5)
    a_log = jnp.clip(2.77 * jax.random.uniform(arg_keys[9], (N, E), jnp.float32) ** levels(arg_keys[9], (N, E), ((1, 4),), -0.2, 0.2), 0.0, 2.77)
    d_skip = jnp.clip(0.5 + 1.0 * jax.random.uniform(arg_keys[10], (E,), jnp.float32) ** levels(arg_keys[10], (E,), ((0, 4),), -0.2, 0.2), 0.5, 1.5)
    w_out = scatter_about(arg_keys[11], (E, D), E ** -0.5, 0.0625, ((0, 4), (1, 64)))
    conv_state = scatter_about(arg_keys[12], (BATCH, K - 1, E), 1.0, 6.0, ((0, 64), (2, 4)))
    ssm_state = scatter_about(arg_keys[13], (BATCH, N, E), 1.0, 6.0, ((0, 64), (2, 4)), jnp.float32)
    lengths = set_ends(jax.random.randint(arg_keys[14], (BATCH,), 0, 6), jax.random.fold_in(arg_keys[14], 1), 0, 5).astype(jnp.int32)
    active_ids = jax.vmap(lambda own: jax.random.permutation(own, SEQ_DEV))(jax.random.split(arg_keys[15], N_DP)).reshape((N_DP, SEQ_DEV)).astype(jnp.int32)
    active_count = draw_active_count(jax.random.fold_in(arg_keys[17], 71), 0)
    return dict(hidden_in=hidden_in, norm_gain=norm_gain, w_in=w_in, conv_w=conv_w, conv_b=conv_b, w_dt_low=w_dt_low, w_bc=w_bc, w_dt=w_dt, dt_bias=dt_bias, a_log=a_log, d_skip=d_skip, w_out=w_out, conv_state=conv_state, ssm_state=ssm_state, lengths=lengths, active_ids=active_ids, active_count=active_count)


def rms_rows(values, epsilon):
    return values * lax.rsqrt(lax.optimization_barrier(jnp.mean(values * values, axis=-1, keepdims=True)) + epsilon)

def active_slots(active_ids, active_count):
    order = jnp.arange(active_ids.shape[-1], dtype=jnp.int32)
    early = order[None, :] < active_count[:, None]
    hits = (active_ids[:, :, None] == order[None, None, :]) & early[:, :, None]
    return jnp.any(hits, axis=1)

def filter_step(conv_state, x_in, lengths, conv_w, conv_b):
    window = jnp.concatenate([conv_state, x_in[:, None, :]], axis=1)
    taps = window.shape[1]
    offsets = jnp.arange(taps, dtype=jnp.int32)
    usable = (lengths[:, None] - (taps - 1) + offsets[None, :] >= 0).astype(jnp.float32)
    summed = lax.optimization_barrier(jnp.sum(window.astype(jnp.float32) * conv_w[None] * usable[:, :, None], axis=1)) + conv_b
    return (window, jax.nn.silu(summed).astype(jnp.bfloat16))

def projections(filtered, w_dt_low, w_bc):
    low = jnp.dot(filtered, w_dt_low, preferred_element_type=jnp.float32)
    both = lax.dot_general(filtered, w_bc, (((1,), (1,)), ((), ())), preferred_element_type=jnp.float32)
    return (low, both)

def step_sizes(low, w_dt, dt_bias):
    low_normed = rms_rows(low, 1e-06).astype(jnp.bfloat16)
    return jax.nn.softplus(jnp.dot(low_normed, w_dt, preferred_element_type=jnp.float32) + dt_bias)

def state_update(state, step_size, b_in, c_out, filtered, z_in, fresh, a_log, d_skip):
    filt_f = filtered.astype(jnp.float32)
    factor = jnp.exp(-step_size[:, None, :] * jnp.exp(a_log)[None])
    updated = factor * state * fresh[:, None, None] + step_size[:, None, :] * b_in[:, :, None] * filt_f[:, None, :]
    output = lax.optimization_barrier(jnp.sum(c_out[:, :, None] * updated, axis=1)) + d_skip * filt_f
    gated = output * jax.nn.silu(z_in.astype(jnp.float32))
    return (updated, gated.astype(jnp.bfloat16))

def reference(hidden_in, norm_gain, w_in, conv_w, conv_b, w_dt_low, w_bc, w_dt, dt_bias, a_log, d_skip, w_out, conv_state, ssm_state, lengths, active_ids, active_count):
    active = active_slots(active_ids, active_count).reshape(-1)
    hidden_f = hidden_in.astype(jnp.float32)
    normed = (rms_rows(hidden_f, 1e-05) * norm_gain).astype(jnp.bfloat16)
    w_flat = w_in.reshape(D, 2, E)
    x_in = jnp.dot(normed, w_flat[:, 0], preferred_element_type=jnp.float32).astype(jnp.bfloat16)
    z_in = jnp.dot(normed, w_flat[:, 1], preferred_element_type=jnp.float32).astype(jnp.bfloat16)
    window, filtered = filter_step(conv_state, x_in, lengths, conv_w, conv_b)
    low, both = projections(filtered, w_dt_low, w_bc)
    b_normed = rms_rows(both[:, :N], 1e-06)
    c_normed = rms_rows(both[:, N:], 1e-06)
    step_size = step_sizes(low, w_dt, dt_bias)
    fresh = (lengths > 0).astype(jnp.float32)

    def grouped(values):
        return values.reshape((N_DP, SEQ_DEV) + values.shape[1:])

    def per_group(items):
        return state_update(*items, a_log, d_skip)
    updated, gated = lax.map(per_group, (grouped(ssm_state), grouped(step_size), grouped(b_normed), grouped(c_normed), grouped(filtered), grouped(z_in), grouped(fresh)))
    updated = updated.reshape(ssm_state.shape)
    gated = gated.reshape(BATCH, E)
    projected = jnp.dot(gated, w_out, preferred_element_type=jnp.float32)
    mixed = (hidden_f + active.astype(jnp.float32)[:, None] * projected).astype(jnp.bfloat16)
    conv_next = jnp.where(active[:, None, None], window[:, 1:], conv_state)
    ssm_next = jnp.where(active[:, None, None], updated, ssm_state)
    return (mixed, conv_next, ssm_next)
```

```python
import functools

import jax
import jax.numpy as jnp
from jax import lax
from jax.experimental import pallas as pl
from jax.experimental.pallas import tpu as pltpu
from jax.sharding import PartitionSpec as P

MESH = pl.DeviceIdType.MESH
BF = jnp.bfloat16
F32 = jnp.float32
NY, NC = 4, 2
ROWS = 24
FRONT_ORDER = ((2, 0), (2, 1), (3, 0), (3, 1), (4, 0), (1, 0), (1, 1), (0, 0))
FRONT_PLAN = ("", "r", "mmtmm", "mdmdmdmddddd")
FRONT_ARRIVAL = ((2, 0), (2, 1), (3, 0), (3, 1), (1, 0), (1, 1), (0, 0), (4, 0))
BACK_ORDER = ((0, 0), (1, 0), (1, 1), (2, 0), (2, 1), (3, 0), (3, 1), (4, 0))
BACK_PLAN = ("mmm", "mmd", "mmdddd", "mddd")


class Geo:
    def __init__(self, n_dp, n_x):
        self.nz = n_dp // (NY * NC)
        self.nm = self.nz * NY
        self.nx = n_x
        dp = lax.axis_index("dp")
        self.x = lax.axis_index("tensor")
        self.c = lax.rem(dp, NC)
        self.m = dp // NC
        self.y = lax.rem(self.m, NY)
        self.z = self.m // NY
        self.sib = NC - 1 - self.c

    def at(self, z, y):
        return ((z * NY + y) * NC + self.c, self.x)

    def at_m(self, m):
        return (m * NC + self.c, self.x)

    def at_x(self, x):
        return (self.m * NC + self.c, x)

    def at_sib(self):
        return (self.m * NC + self.sib, self.x)


def rcopy(src, dst, send, recv, dev):
    return pltpu.make_async_remote_copy(
        src_ref=src, dst_ref=dst, send_sem=send, recv_sem=recv, device_id=dev, device_id_type=MESH
    )


def greet(g):
    sem = pltpu.get_barrier_semaphore()
    devs = [g.at(lax.rem(g.z + dz, g.nz), lax.rem(g.y + e, NY)) for dz in (1, g.nz - 1) for e in range(NY)]
    devs += [g.at(g.z, lax.rem(g.y + e, NY)) for e in range(1, NY)]
    devs += [g.at_x(lax.rem(g.x + e, g.nx)) for e in range(1, g.nx)]
    devs.append(g.at_sib())
    for dev in devs:
        pl.semaphore_signal(sem, inc=1, device_id=dev, device_id_type=MESH)
    return len(devs)


def greeted(count):
    pl.semaphore_wait(pltpu.get_barrier_semaphore(), count)


def slots(ids_ref, count_ref):
    n = ids_ref.shape[1]
    slot = lax.broadcasted_iota(jnp.int32, (n, n), 0)
    order = lax.broadcasted_iota(jnp.int32, (n, n), 1)
    live = jnp.logical_and(order < count_ref[0], order < ROWS)
    hit = jnp.logical_and(slot == jnp.broadcast_to(ids_ref[...], (n, n)), live)
    sel = jnp.where(hit, 1.0, 0.0).astype(F32)
    return sel


def all_in(ref, sem, g):
    rcopy(ref, ref, sem, sem, g.at_sib()).wait_recv()


def stage(g, a, w2d, part, got, summed, own, peer, n_peer, sems, y_src, k1, k2, muls, plan, after_start, relay=None):
    send, ry, r1, r2, rf, rs, ar = sems
    s_ref, x_ref = summed
    nz = g.nz
    far = nz // 2
    half = NY // 2
    first = jnp.where(lax.rem(g.z, far) >= far // 2, 0, 1)
    dirs = (first, 1 - first)

    def rows(q):
        return pl.ds(pl.multiple_of(q * ROWS, 8), ROWS)

    def blk(grp, d):
        return a.at[grp, rows(lax.rem(g.y + d, NY)), pl.ds(0, k1)]

    def blk2(grp, d):
        return a.at[grp, rows(lax.rem(g.y + d, NY)), pl.ds(k1, k2)]

    def group(s, q):
        if s == 0:
            return g.z, 0
        return lax.rem(g.z + nz + (2 * q - 1) * s, nz), (s + q * far if s < far else far)

    def seen_by(s, q):
        if s == 0 or s == far:
            return s
        return s + (1 - q) * far

    def next_z(q):
        return lax.rem(g.z + nz + 1 - 2 * q, nz)

    def ring(s, q, i, grp):
        d = lax.rem(half * q + i, NY)
        return rcopy(blk(grp, d), blk(grp, d), send.at[0], r1.at[q, s - 1, d], g.at(next_z(q), g.y))

    def ring2(s, q, grp):
        return rcopy(blk2(grp, 0), blk2(grp, 0), send.at[1], r2.at[q, s - 1], g.at(next_z(q), g.y))

    def fan(grp, gi, e):
        dev = g.at(g.z, lax.rem(g.y + e, NY))
        return rcopy(blk2(grp, 0), blk2(grp, 0), send.at[1], rf.at[gi - 1], dev)

    def multiply(s, q):
        grp, gi = group(s, q)
        if s == 0:
            all_in(a.at[g.z, pl.ds(0, (NY - 1) * ROWS)], ry, g)
        elif k2:
            all_in(a.at[grp, pl.ds(0, (NY - 1) * ROWS), pl.ds(k1, k2)], rf.at[gi - 1], g)
        res = lax.dot_general(a[grp], w2d(), (((1,), (1,)), ((), ())), preferred_element_type=F32)
        for j in range(n_peer):
            part[j, grp] = res[:, j * 128 : (j + 1) * 128].astype(BF)
        for e in range(1, n_peer):
            j = lax.rem(own + e, n_peer)
            rcopy(part.at[j, grp], got.at[e - 1, grp], send.at[2], rs.at[gi], peer(j)).start()

    def drain(s, q):
        grp, gi = group(s, q)
        all_in(got.at[:, grp], rs.at[gi], g)
        total = part[own, grp].astype(F32)
        for e in range(1, n_peer):
            total = total + got[e - 1, grp].astype(F32)
        s_ref[grp] = total.astype(BF)
        for d in range(NY):
            y = lax.rem(g.y + d, NY)
            if s == 0 and d == 0:
                x_ref[g.m] = s_ref[grp, rows(y)]
            else:
                sem = ar.at[seen_by(s, q)]
                rcopy(s_ref.at[grp, rows(y)], x_ref.at[g.m], send.at[3], sem, g.at(grp, y)).start()

    mine = rows(g.y)
    for q in dirs:
        if k2:
            ring2(1, q, g.z).start()
    for e in range(NY):
        for q in dirs:
            src = y_src(e)
            dst = a.at[g.z, mine, pl.ds(0, k1)]
            dev = g.at(next_z(q), lax.rem(g.y + e, NY))
            rcopy(src.at[:, pl.ds(0, k1)], dst, send.at[0], r1.at[q, 0, (NY - e) % NY], dev).start()
    for e in range(1, NY):
        rcopy(y_src(e), a.at[g.z, mine], send.at[4], ry, g.at(g.z, lax.rem(g.y + e, NY))).start()
    after_start()

    to_multiply = [(s, dirs[i] if s < far else 0) for s, i in muls]
    to_drain = list(to_multiply)

    def turn(s):
        for q in dirs if s < far else (0,):
            grp, gi = group(s, q)
            ring2(s, q, grp).wait_recv()
            if s + 1 < far:
                ring2(s + 1, q, grp).start()
            elif s < far:

                @pl.when(q == 0)
                def _():
                    ring2(far, 0, grp).start()

            for e in range(1, NY):
                fan(grp, gi, e).start()

    for s in range(1, far + 1):
        if k2 and s < far:
            turn(s)
        for i in range(NY if s < far else half):
            for q in dirs:
                grp, gi = group(s, q)
                ring(s, q, i, grp).wait_recv()
                if s + 1 < far or (s < far and i < half):
                    ring(s + 1, q, i, grp).start()
        for what in plan[s - 1]:
            if what == "m":
                multiply(*to_multiply.pop(0))
            elif what == "d":
                drain(*to_drain.pop(0))
            elif what == "r":
                relay()
            else:
                turn(far)

    def arrived(s, i):
        q = dirs[i] if s < far else 0
        grp, gi = group(s, q)
        n = NY if s else NY - 1
        all_in(x_ref.at[pl.ds(grp * NY, n)], ar.at[gi], g)
        return grp

    def finish():
        def sent(ref, i):
            rcopy(ref, ref, send.at[i], ry, g.at_sib()).wait_send()

        sent(a.at[pl.ds(0, nz - 1), :, pl.ds(0, k1)], 0)
        if k2:
            sent(a.at[pl.ds(0, nz - 1), :, pl.ds(k1, k2)], 1)
        sent(got, 2)
        sent(x_ref.at[pl.ds(0, g.nm - 1)], 3)
        sent(a.at[0, pl.ds(0, (NY - 1) * ROWS)], 4)

    return arrived, finish


class Weights:
    def __init__(self, g, n, me, dev, src, dst, sems, local):
        self.g, self.n, self.me, self.dev, self.src, self.dst = g, n, me, dev, src, dst
        self.ws, self.wr = sems
        self.load = pltpu.make_async_copy(src(me), dst(me, g.c), local)
        self.ready = False

    def start(self):
        for e in range(1, self.n):
            j = lax.rem(self.me + e, self.n)
            rcopy(self.src(j), self.dst(self.me, self.g.c), self.ws.at[0], self.wr.at[0], self.dev(j)).start()
        own = self.dst(self.me, self.g.c)
        rcopy(self.src(self.me), own, self.ws.at[1], self.wr.at[1], self.g.at_sib()).start()

    def relay(self, three):
        all_in(three, self.wr.at[0], self.g)
        for e in range(1, self.n):
            blk = self.dst(lax.rem(self.me + e, self.n), self.g.c)
            rcopy(blk, blk, self.ws.at[1], self.wr.at[1], self.g.at_sib()).start()

    def wait(self, four):
        if self.ready:
            return
        self.ready = True
        self.load.wait()
        all_in(four, self.wr.at[1], self.g)

    def finish(self, three, four):
        for i, ref in enumerate((three, four)):
            rcopy(ref, ref, self.ws.at[i], self.wr.at[i], self.g.at_sib()).wait_send()


def rms(v, eps):
    return v * lax.rsqrt(jnp.mean(v * v, axis=-1, keepdims=True) + eps)


def softplus(v):
    return jnp.maximum(v, 0.0) + jnp.log1p(jnp.exp(-jnp.abs(v)))


def silu(v):
    return v / (1.0 + jnp.exp(-v))


def front_kernel(
    n_dp, n_x,
    hidden, gain, wt, convw, convb, wlow_h, wbc_h, wdt_h, dtb, conv_h, lens, wo, ids, count,
    xs_out, z_out, filt_out, step_out, meta_out, w2_out,
    a, w, part, got, s_ref, x_ref, lb, lgot, wlow, wbc, wdt, conv, acc_low, acc_bc, w2,
    ws2, wr2, ws, wr, send, ry, r1, r2, rf, rs, ar, ls, lr, local,
):
    g = Geo(n_dp, n_x)
    ks = hidden.shape[1] // n_x
    friends = greet(g)
    cols = pl.ds(pl.multiple_of(g.x * ks, 128), ks)
    loads = [
        pltpu.make_async_copy(src, dst, local.at[i + 1])
        for i, (src, dst) in enumerate(((conv_h, conv), (wlow_h, wlow), (wbc_h, wbc), (wdt_h, wdt)))
    ]
    weights = Weights(
        g, n_x, g.x, g.at_x, lambda j: wt.at[:, :, pl.ds(pl.multiple_of(j * ks, 128), ks)],
        lambda j, c: w.at[j, :, c], (ws, wr), local.at[0],
    )
    w_three, w_four = w.at[pl.ds(0, n_x - 1), :, 0], w.at[:, :, 0]
    weights.load.start()

    sel_t = slots(ids, count)
    sel = jnp.transpose(sel_t)[:ROWS].astype(BF)
    sel_tb = sel_t[:, :ROWS].astype(BF)
    h = hidden[...].astype(F32)
    scale = lax.rsqrt(jnp.mean(h * h, axis=-1, keepdims=True) + 1e-05)
    normed = (hidden[:, cols].astype(F32) * scale * gain[:, cols]).astype(BF)
    my_rows = pl.ds(pl.multiple_of(g.y * ROWS, 8), ROWS)
    a[g.z, my_rows] = jnp.dot(sel, normed, preferred_element_type=F32).astype(BF)
    greeted(friends)

    weights.start()

    def load_all():
        for load in loads:
            load.start()

    def w2d():
        weights.wait(w_four)
        return w[...].reshape(n_x * 128, ks)

    arrived, finish = stage(
        g, a, w2d, part, got, (s_ref, x_ref), g.x, g.at_x, n_x, (send, ry, r1, r2, rf, rs, ar),
        lambda e: a.at[g.z, my_rows], ks // 2, ks // 2, FRONT_ORDER, FRONT_PLAN, load_all,
        lambda: weights.relay(w_three),
    )
    k2 = wo.shape[1] // NY
    out_weights = Weights(
        g, NY, g.y, lambda j: g.at(g.z, j), lambda j: wo.at[:, pl.ds(pl.multiple_of(j * k2, 128), k2)],
        lambda j, c: w2.at[j, c], (ws2, wr2), local.at[0],
    )
    w2_three, w2_four = w2.at[pl.ds(0, NY - 1), 0], w2.at[:, 0]
    out_weights.load.start()
    out_weights.start()
    for load in loads:
        load.wait()

    n = ids.shape[1]
    eye = lax.broadcasted_iota(jnp.int32, (n, n), 0) == lax.broadcasted_iota(jnp.int32, (n, n), 1)
    length = jnp.sum(
        jnp.where(eye, jnp.broadcast_to(lens[...].astype(F32), (n, n)), 0.0), axis=1, keepdims=True
    )
    taps = convw.shape[0]
    usable = [jnp.where(length >= float(taps - 1 - k), 1.0, 0.0) for k in range(taps - 1)]
    lane = lax.broadcasted_iota(jnp.int32, (ROWS, 128), 1)
    span = NY * 64
    acc_low[...] = jnp.zeros_like(acc_low)
    acc_bc[...] = jnp.zeros_like(acc_bc)
    for one in FRONT_ARRIVAL:
        grp = arrived(*one)
        ch = pl.ds(pl.multiple_of(grp * span, span), span)
        x_parts, z_parts = [], []
        for p in range(NY // 2):
            b0 = x_ref[grp * NY + 2 * p].astype(F32)
            b1 = x_ref[grp * NY + 2 * p + 1].astype(F32)
            x_parts.append(jnp.where(lane < 64, b0, pltpu.roll(b1, 64, 1)))
            z_parts.append(jnp.where(lane < 64, pltpu.roll(b0, 64, 1), b1))
        x_c = jnp.concatenate(x_parts, axis=1).astype(BF)
        z_c = jnp.concatenate(z_parts, axis=1).astype(BF)
        xs = jnp.dot(sel_tb, x_c, preferred_element_type=F32)
        zs = jnp.dot(sel_tb, z_c, preferred_element_type=F32)
        xs_out[:, ch] = xs.astype(BF)
        z_out[:, ch] = silu(zs)
        total = xs * convw[taps - 1 : taps, ch]
        for k in range(taps - 1):
            total = total + conv[k, :, ch].astype(F32) * (convw[k : k + 1, ch] * usable[k])
        filt = silu(total + convb[:, ch]).astype(BF)
        filt_out[:, ch] = filt.astype(F32)
        acc_low[...] += jnp.dot(filt, wlow[ch, :], preferred_element_type=F32)
        acc_bc[...] += lax.dot_general(
            filt, wbc[:, ch], (((1,), (1,)), ((), ())), preferred_element_type=F32
        )

    rank = wlow.shape[1]
    nb = wbc.shape[0]
    lb[...] = jnp.zeros_like(lb)
    lb[:, :rank] = acc_low[...].astype(BF)
    lb[:, rank : rank + nb] = acc_bc[...].astype(BF)

    for e in range(1, n_x):
        rcopy(lb, lgot.at[e - 1], ls, lr, g.at_x(lax.rem(g.x + e, n_x))).start()
    out_weights.relay(w2_three)
    acc = lb[...].astype(F32)
    all_in(lgot, lr, g)
    for e in range(1, n_x):
        acc = acc + lgot[e - 1].astype(F32)
    out_weights.wait(w2_four)
    w2_out[...] = w2[...]
    low = rms(acc[:, :rank], 1e-06).astype(BF)
    step_out[...] = softplus(jnp.dot(low, wdt[...], preferred_element_type=F32) + dtb[...])
    bc = acc[:, rank : rank + 128]
    li = lax.broadcasted_iota(jnp.int32, bc.shape, 1)
    half = nb // 2
    is_b = li < half
    is_c = jnp.logical_and(li >= half, li < nb)
    sq = bc * bc
    mb = jnp.sum(jnp.where(is_b, sq, 0.0), axis=1, keepdims=True) * (1.0 / half)
    mc = jnp.sum(jnp.where(is_c, sq, 0.0), axis=1, keepdims=True) * (1.0 / half)
    live = jnp.sum(sel_t, axis=1, keepdims=True)
    fresh = jnp.where(length > 0.0, 1.0, 0.0)
    meta = bc * jnp.where(is_b, lax.rsqrt(mb + 1e-06), lax.rsqrt(mc + 1e-06))
    meta = jnp.where(li == nb, live, meta)
    meta_out[...] = jnp.where(li == nb + 1, fresh, meta)

    rcopy(lgot, lgot, ls, lr, g.at_sib()).wait_send()
    weights.finish(w_three, w_four)
    out_weights.finish(w2_three, w2_four)
    finish()


def state_kernel(ids, count, xs, zg, filt, step, meta, alog, dskip, conv, state, gated, conv_next, state_next, rate, act, gated_f):
    per = state.shape[0]
    n_state = state.shape[1]
    width = state.shape[2]

    @pl.when(pl.program_id(0) == 0)
    def _():
        rate[...] = -jnp.exp(alog[...])
        for s in range(ids.shape[1]):
            act[s] = 0

        def mark(k, carry):
            act[ids[0, k]] = 1
            return carry

        lax.fori_loop(0, count[0], mark, 0)

    live = meta[:, 2 * n_state : 2 * n_state + 1] > 0.5
    window = [conv[1], conv[2], xs[...]]
    for k in range(3):
        conv_next[k] = jnp.where(live, window[k].astype(F32), conv[k].astype(F32)).astype(BF)

    row_i = lax.broadcasted_iota(jnp.int32, (n_state, 128), 0)
    lane_i = lax.broadcasted_iota(jnp.int32, (n_state, 128), 1)
    chunk = 512
    gated_f[...] = jnp.zeros_like(gated_f)

    def one(s, carry):
        on = act[pl.program_id(0) * per + s]

        @pl.when(on == 0)
        def _():
            state_next[s] = state[s]

        @pl.when(on != 0)
        def _():
            mrow = jnp.broadcast_to(meta[pl.ds(s, 1), :], (n_state, 128))
            b = jnp.sum(jnp.where(lane_i == row_i, mrow, 0.0), axis=1, keepdims=True)
            cc = jnp.sum(jnp.where(lane_i == row_i + n_state, mrow, 0.0), axis=1, keepdims=True)
            fresh = jnp.sum(jnp.where(lane_i == 2 * n_state + 1, mrow, 0.0), axis=1, keepdims=True)
            for t in range(width // chunk):
                sl = slice(t * chunk, (t + 1) * chunk)
                st = step[pl.ds(s, 1), sl]
                f = filt[pl.ds(s, 1), sl]
                upd = jnp.exp(rate[:, sl] * st) * (state[s, :, sl] * fresh) + b * (st * f)
                state_next[s, :, sl] = upd
                y = jnp.sum(cc * upd, axis=0, keepdims=True) + dskip[:, sl] * f
                gated_f[pl.ds(s, 1), sl] = y * zg[pl.ds(s, 1), sl]

        return carry

    lax.fori_loop(0, per, one, 0)
    gated[...] = gated_f[...].astype(BF)


def back_kernel(
    n_dp, n_x,
    hidden_h, gated, w_h, ids, count,
    mixed,
    a, part, got, s_ref, x_ref, gc, px, hidden, w,
    send, ry, r1, r2, rf, rs, ar, ls, lr, local,
):
    g = Geo(n_dp, n_x)
    ks = gated.shape[1] // NY
    friends = greet(g)
    share = pl.ds(pl.multiple_of(g.x * mixed.shape[1], 128), mixed.shape[1])
    loads = (
        pltpu.make_async_copy(w_h, w, local.at[0]),
        pltpu.make_async_copy(hidden_h.at[:, share], hidden, local.at[1]),
    )
    for load in loads:
        load.start()
    cols = pl.ds(pl.multiple_of(g.y * ks, 128), ks)
    my_rows = pl.ds(pl.multiple_of(g.y * ROWS, 8), ROWS)
    sel_t = slots(ids, count)
    sel = jnp.transpose(sel_t)[:ROWS].astype(BF)
    gc[...] = jnp.dot(sel, gated[...], preferred_element_type=F32).astype(BF)
    a[g.z, my_rows] = gc[:, cols]
    greeted(friends)

    def y_src(e):
        return gc.at[:, pl.ds(pl.multiple_of(lax.rem(g.y + e, NY) * ks, 128), ks)]

    def w2d():
        return w[...].reshape(NY * 128, ks)

    def loaded():
        for load in loads:
            load.wait()

    arrived, finish = stage(
        g, a, w2d, part, got, (s_ref, x_ref), g.y, lambda j: g.at(g.z, j), NY,
        (send, ry, r1, r2, rf, rs, ar), y_src, ks, 0, BACK_ORDER, BACK_PLAN, loaded,
    )
    per = g.nm // n_x
    for one in BACK_ORDER:
        grp = arrived(*one)
        j = grp * NY // per
        e = lax.rem(j + n_x - g.x, n_x)

        @pl.when(e != 0)
        def _():
            blks = x_ref.at[pl.ds(grp * NY, NY)]
            rcopy(blks, px.at[e - 1, pl.ds(grp * NY - j * per, NY)], ls, lr, g.at_x(j)).start()

    all_in(px, lr, g)
    for k in range(per):
        total = x_ref[g.x * per + k].astype(F32)
        for e in range(1, n_x):
            total = total + px[e - 1, k].astype(F32)
        spread = lax.dot_general(
            sel_t[:, :ROWS], total, (((1,), (0,)), ((), ())),
            precision=lax.Precision.HIGHEST, preferred_element_type=F32,
        )
        base = hidden[:, k * 128 : (k + 1) * 128].astype(F32)
        mixed[:, k * 128 : (k + 1) * 128] = (base + spread).astype(BF)

    rcopy(px, px, ls, lr, g.at_sib()).wait_send()
    finish()


def stage_scratch(nz, n_peer, ks):
    nm = nz * NY
    blk = NY * ROWS
    return [
        pltpu.VMEM((n_peer, nz, blk, 128), BF),
        pltpu.VMEM((n_peer - 1, nz, blk, 128), BF),
        pltpu.VMEM((nz, blk, 128), BF),
        pltpu.VMEM((nm, ROWS, 128), BF),
    ]


def stage_sems(nz):
    dma = pltpu.SemaphoreType.DMA
    far = nz // 2
    return [
        dma((5,)), dma, dma((2, far, NY)), dma((2, far)), dma((nz - 1,)), dma((nz,)),
        dma((nz,)), dma, dma,
    ]


def in_hbm(v):
    return pltpu.with_memory_space_constraint(v, pltpu.HBM)


def body(
    n_dp, n_x,
    hidden_in, norm_gain, w_in, conv_w, conv_b, w_dt_low, w_bc, w_dt, dt_bias, a_log, d_skip, w_out,
    conv_state, ssm_state, lengths, active_ids, active_count,
):
    n_slot, depth = hidden_in.shape
    width = conv_w.shape[1]
    nz = n_dp // (NY * NC)
    ka = depth // n_x
    kc = width // NY
    vm = pl.BlockSpec(memory_space=pltpu.VMEM)
    sm = pl.BlockSpec(memory_space=pltpu.SMEM)
    hbm = pl.BlockSpec(memory_space=pltpu.HBM)
    wt = jnp.transpose(w_in, (1, 2, 3, 0)).reshape(2, w_in.shape[3], depth)
    wo = jnp.transpose(w_out)
    conv_t = jnp.transpose(conv_state, (1, 0, 2))
    sds = jax.ShapeDtypeStruct
    blk = NY * ROWS

    xs, zg, filt, step, meta, w2 = pl.pallas_call(
        functools.partial(front_kernel, n_dp, n_x),
        name="front",
        out_shape=(
            sds((n_slot, width), BF), sds((n_slot, width), F32), sds((n_slot, width), F32),
            sds((n_slot, width), F32), sds((n_slot, 128), F32), sds((NY, NC, wo.shape[0], kc), BF),
        ),
        in_specs=[vm, vm, hbm, vm, vm, hbm, hbm, hbm, vm, hbm, vm, hbm, vm, sm],
        out_specs=(vm,) * 6,
        scratch_shapes=[
            pltpu.VMEM((nz, blk, ka), BF),
            pltpu.VMEM((n_x, 2, NC, w_in.shape[3], ka), BF),
            *stage_scratch(nz, n_x, ka),
            pltpu.VMEM((n_slot, w_dt_low.shape[1] + 128), BF),
            pltpu.VMEM((n_x - 1, n_slot, w_dt_low.shape[1] + 128), BF),
            pltpu.VMEM(w_dt_low.shape, BF),
            pltpu.VMEM(w_bc.shape, BF),
            pltpu.VMEM(w_dt.shape, BF),
            pltpu.VMEM(conv_t.shape, BF),
            pltpu.VMEM((n_slot, w_dt_low.shape[1]), F32),
            pltpu.VMEM((n_slot, w_bc.shape[0]), F32),
            pltpu.VMEM((NY, NC, wo.shape[0], kc), BF),
            *[pltpu.SemaphoreType.DMA((2,))] * 4,
            *stage_sems(nz),
            pltpu.SemaphoreType.DMA((5,)),
        ],
        compiler_params=pltpu.CompilerParams(collective_id=0, has_side_effects=True, vmem_limit_bytes=18 << 20),
        cost_estimate=pl.CostEstimate(flops=20_000_000_000, bytes_accessed=4_000_000, transcendentals=0),
    )(
        *map(
            in_hbm,
            (
                hidden_in, norm_gain.reshape(1, depth), wt, conv_w, conv_b.reshape(1, width), w_dt_low, w_bc, w_dt,
                dt_bias.reshape(1, width), conv_t, lengths.reshape(1, n_slot), wo, active_ids,
            ),
        ),
        active_count,
    )

    per = 8
    n_state = a_log.shape[0]

    def row(shape):
        return pl.BlockSpec(shape, lambda i: (i,) + (0,) * (len(shape) - 1))

    def full(shape):
        return pl.BlockSpec(shape, lambda i: (0,) * len(shape))

    conv_spec = pl.BlockSpec((3, per, width), lambda i: (0, i, 0))
    gated, conv_next, ssm_next = pl.pallas_call(
        state_kernel,
        name="state",
        grid=(n_slot // per,),
        out_shape=(
            sds((n_slot, width), BF), sds((3, n_slot, width), BF), sds(ssm_state.shape, F32),
        ),
        in_specs=[
            sm, sm, row((per, width)), row((per, width)), row((per, width)), row((per, width)), row((per, 128)),
            full((n_state, width)), full((1, width)), conv_spec, row((per, n_state, width)),
        ],
        out_specs=(row((per, width)), conv_spec, row((per, n_state, width))),
        scratch_shapes=[
            pltpu.VMEM((n_state, width), F32), pltpu.SMEM((n_slot,), jnp.int32), pltpu.VMEM((per, width), F32),
        ],
        compiler_params=pltpu.CompilerParams(vmem_limit_bytes=16 << 20),
        cost_estimate=pl.CostEstimate(flops=20_000_000, bytes_accessed=8_000_000, transcendentals=800_000),
    )(active_ids, active_count, xs, zg, filt, step, meta, a_log, d_skip.reshape(1, width), conv_t, ssm_state)

    mixed = pl.pallas_call(
        functools.partial(back_kernel, n_dp, n_x),
        name="back",
        out_shape=sds((n_slot, depth // n_x), BF),
        in_specs=[hbm, vm, hbm, vm, sm],
        out_specs=vm,
        scratch_shapes=[
            pltpu.VMEM((nz, blk, kc), BF),
            *stage_scratch(nz, NY, kc),
            pltpu.VMEM((ROWS, width), BF),
            pltpu.VMEM((n_x - 1, nz * NY // n_x, ROWS, 128), BF),
            pltpu.VMEM((n_slot, depth // n_x), BF),
            pltpu.VMEM(w2.shape, BF),
            *stage_sems(nz),
            pltpu.SemaphoreType.DMA((2,)),
        ],
        compiler_params=pltpu.CompilerParams(collective_id=1, has_side_effects=True, vmem_limit_bytes=18 << 20),
        cost_estimate=pl.CostEstimate(flops=20_000_000_000, bytes_accessed=4_000_000, transcendentals=0),
    )(hidden_in, gated, w2, active_ids, active_count)
    return (mixed, jnp.transpose(conv_next, (1, 0, 2)), ssm_next)


def solution(mesh):
    in_specs = (
        P("dp", None),
        P(),
        P(None, None, "tensor", "dp"),
        P(None, "tensor"),
        P("tensor"),
        P("tensor", None),
        P(None, "tensor"),
        P(None, "tensor"),
        P("tensor"),
        P(None, "tensor"),
        P("tensor"),
        P("tensor", "dp"),
        P("dp", None, "tensor"),
        P("dp", None, "tensor"),
        P("dp"),
        P("dp", None),
        P("dp"),
    )
    out_specs = (P("dp", "tensor"), P("dp", None, "tensor"), P("dp", None, "tensor"))
    run = functools.partial(body, mesh.shape["dp"], mesh.shape["tensor"])
    return jax.shard_map(run, mesh=mesh, in_specs=in_specs, out_specs=out_specs, check_vma=False)
```

```python
import functools

import jax
import jax.numpy as jnp
from jax import lax
from jax.experimental import pallas as pl
from jax.experimental.pallas import tpu as pltpu
from jax.sharding import PartitionSpec as P

MESH = pl.DeviceIdType.MESH
BF = jnp.bfloat16
F32 = jnp.float32
NY, NC = 4, 2
ROWS = 24
FRONT_ORDER = ((2, 0), (2, 1), (3, 0), (3, 1), (4, 0), (1, 0), (1, 1), (0, 0))
FRONT_PLAN = ("", "r", "tmmmm", "mdmdmdmddcdcdd")
FRONT_ARRIVAL = ((2, 0), (2, 1), (3, 0), (3, 1), (1, 0), (1, 1), (0, 0), (4, 0))
BACK_ORDER = ((0, 0), (1, 0), (1, 1), (2, 0), (2, 1), (3, 0), (3, 1), (4, 0))
BACK_PLAN = ("mmm", "mmd", "mmdddd", "mddd")


class Geo:
    def __init__(self, n_dp, n_x):
        self.nz = n_dp // (NY * NC)
        self.nm = self.nz * NY
        self.nx = n_x
        dp = lax.axis_index("dp")
        self.x = lax.axis_index("tensor")
        self.c = lax.rem(dp, NC)
        self.m = dp // NC
        self.y = lax.rem(self.m, NY)
        self.z = self.m // NY
        self.sib = NC - 1 - self.c

    def at(self, z, y):
        return ((z * NY + y) * NC + self.c, self.x)

    def at_m(self, m):
        return (m * NC + self.c, self.x)

    def at_x(self, x):
        return (self.m * NC + self.c, x)

    def at_sib(self):
        return (self.m * NC + self.sib, self.x)


def rcopy(src, dst, send, recv, dev):
    return pltpu.make_async_remote_copy(
        src_ref=src, dst_ref=dst, send_sem=send, recv_sem=recv, device_id=dev, device_id_type=MESH
    )


def greet(g):
    sem = pltpu.get_barrier_semaphore()
    devs = [g.at(lax.rem(g.z + dz, g.nz), lax.rem(g.y + e, NY)) for dz in (1, g.nz - 1) for e in range(NY)]
    devs += [g.at(g.z, lax.rem(g.y + e, NY)) for e in range(1, NY)]
    devs += [g.at_x(lax.rem(g.x + e, g.nx)) for e in range(1, g.nx)]
    devs.append(g.at_sib())
    for dev in devs:
        pl.semaphore_signal(sem, inc=1, device_id=dev, device_id_type=MESH)
    return len(devs)


def greeted(count):
    pl.semaphore_wait(pltpu.get_barrier_semaphore(), count)


def slots(ids_ref, count_ref):
    n = ids_ref.shape[1]
    slot = lax.broadcasted_iota(jnp.int32, (n, n), 0)
    order = lax.broadcasted_iota(jnp.int32, (n, n), 1)
    live = jnp.logical_and(order < count_ref[0], order < ROWS)
    hit = jnp.logical_and(slot == jnp.broadcast_to(ids_ref[...], (n, n)), live)
    sel = jnp.where(hit, 1.0, 0.0).astype(F32)
    return sel


def all_in(ref, sem, g):
    rcopy(ref, ref, sem, sem, g.at_sib()).wait_recv()


def stage(g, a, w2d, part, got, summed, own, peer, n_peer, sems, y_src, k1, k2, muls, plan, after_start, relay=None, consume=None):
    send, ry, r1, r2, rf, rs, ar = sems
    s_ref, x_ref = summed
    nz = g.nz
    far = nz // 2
    half = NY // 2
    first = jnp.where(lax.rem(g.z, far) >= far // 2, 0, 1)
    dirs = (first, 1 - first)

    def rows(q):
        return pl.ds(pl.multiple_of(q * ROWS, 8), ROWS)

    def blk(grp, d):
        return a.at[grp, rows(lax.rem(g.y + d, NY)), pl.ds(0, k1)]

    def blk2(grp, d):
        return a.at[grp, rows(lax.rem(g.y + d, NY)), pl.ds(k1, k2)]

    def group(s, q):
        if s == 0:
            return g.z, 0
        return lax.rem(g.z + nz + (2 * q - 1) * s, nz), (s + q * far if s < far else far)

    def seen_by(s, q):
        if s == 0 or s == far:
            return s
        return s + (1 - q) * far

    def next_z(q):
        return lax.rem(g.z + nz + 1 - 2 * q, nz)

    def ring(s, q, i, grp):
        d = lax.rem(half * q + i, NY)
        return rcopy(blk(grp, d), blk(grp, d), send.at[0], r1.at[q, s - 1, d], g.at(next_z(q), g.y))

    def ring2(s, q, grp):
        return rcopy(blk2(grp, 0), blk2(grp, 0), send.at[1], r2.at[q, s - 1], g.at(next_z(q), g.y))

    def fan(grp, gi, e):
        dev = g.at(g.z, lax.rem(g.y + e, NY))
        return rcopy(blk2(grp, 0), blk2(grp, 0), send.at[1], rf.at[gi - 1], dev)

    def multiply(s, q):
        grp, gi = group(s, q)
        if s == 0:
            all_in(a.at[g.z, pl.ds(0, (NY - 1) * ROWS)], ry, g)
        elif k2:
            all_in(a.at[grp, pl.ds(0, (NY - 1) * ROWS), pl.ds(k1, k2)], rf.at[gi - 1], g)
        res = lax.dot_general(a[grp], w2d(), (((1,), (1,)), ((), ())), preferred_element_type=F32)
        for j in range(n_peer):
            part[j, grp] = res[:, j * 128 : (j + 1) * 128].astype(BF)
        for e in range(1, n_peer):
            j = lax.rem(own + e, n_peer)
            rcopy(part.at[j, grp], got.at[e - 1, grp], send.at[2], rs.at[gi], peer(j)).start()

    def drain(s, q):
        grp, gi = group(s, q)
        all_in(got.at[:, grp], rs.at[gi], g)
        total = part[own, grp].astype(F32)
        for e in range(1, n_peer):
            total = total + got[e - 1, grp].astype(F32)
        s_ref[grp] = total.astype(BF)
        for d in range(NY):
            y = lax.rem(g.y + d, NY)
            if s == 0 and d == 0:
                x_ref[g.m] = s_ref[grp, rows(y)]
            else:
                sem = ar.at[seen_by(s, q)]
                rcopy(s_ref.at[grp, rows(y)], x_ref.at[g.m], send.at[3], sem, g.at(grp, y)).start()

    mine = rows(g.y)
    for q in dirs:
        if k2:
            ring2(1, q, g.z).start()
    for e in range(NY):
        for q in dirs:
            src = y_src(e)
            dst = a.at[g.z, mine, pl.ds(0, k1)]
            dev = g.at(next_z(q), lax.rem(g.y + e, NY))
            rcopy(src.at[:, pl.ds(0, k1)], dst, send.at[0], r1.at[q, 0, (NY - e) % NY], dev).start()
    for e in range(1, NY):
        rcopy(y_src(e), a.at[g.z, mine], send.at[4], ry, g.at(g.z, lax.rem(g.y + e, NY))).start()
    after_start()

    def arrived(s, i):
        q = dirs[i] if s < far else 0
        grp, gi = group(s, q)
        n = NY if s else NY - 1
        all_in(x_ref.at[pl.ds(grp * NY, n)], ar.at[gi], g)
        return grp

    to_multiply = [(s, dirs[i] if s < far else 0) for s, i in muls]
    to_drain = list(to_multiply)

    def turn(s):
        for q in dirs if s < far else (0,):
            grp, gi = group(s, q)
            ring2(s, q, grp).wait_recv()
            if s + 1 < far:
                ring2(s + 1, q, grp).start()
            elif s < far:

                @pl.when(q == 0)
                def _():
                    ring2(far, 0, grp).start()

            for e in range(1, NY):
                fan(grp, gi, e).start()

    for s in range(1, far + 1):
        if k2 and s < far:
            turn(s)
        for i in range(NY if s < far else half):
            for q in dirs:
                grp, gi = group(s, q)
                ring(s, q, i, grp).wait_recv()
                if s + 1 < far or (s < far and i < half):
                    ring(s + 1, q, i, grp).start()
        for what in plan[s - 1]:
            if what == "m":
                multiply(*to_multiply.pop(0))
            elif what == "d":
                drain(*to_drain.pop(0))
            elif what == "r":
                relay()
            elif what == "c":
                consume(arrived)
            else:
                turn(far)

    def finish():
        def sent(ref, i):
            rcopy(ref, ref, send.at[i], ry, g.at_sib()).wait_send()

        sent(a.at[pl.ds(0, nz - 1), :, pl.ds(0, k1)], 0)
        if k2:
            sent(a.at[pl.ds(0, nz - 1), :, pl.ds(k1, k2)], 1)
        sent(got, 2)
        sent(x_ref.at[pl.ds(0, g.nm - 1)], 3)
        sent(a.at[0, pl.ds(0, (NY - 1) * ROWS)], 4)

    return arrived, finish


class Weights:
    def __init__(self, g, n, me, dev, src, dst, sems, local):
        self.g, self.n, self.me, self.dev, self.src, self.dst = g, n, me, dev, src, dst
        self.ws, self.wr = sems
        self.load = pltpu.make_async_copy(src(me), dst(me, g.c), local)
        self.ready = False

    def start(self):
        for e in range(1, self.n):
            j = lax.rem(self.me + e, self.n)
            rcopy(self.src(j), self.dst(self.me, self.g.c), self.ws.at[0], self.wr.at[0], self.dev(j)).start()
        own = self.dst(self.me, self.g.c)
        rcopy(self.src(self.me), own, self.ws.at[1], self.wr.at[1], self.g.at_sib()).start()

    def relay(self, three):
        all_in(three, self.wr.at[0], self.g)
        for e in range(1, self.n):
            blk = self.dst(lax.rem(self.me + e, self.n), self.g.c)
            rcopy(blk, blk, self.ws.at[1], self.wr.at[1], self.g.at_sib()).start()

    def wait(self, four):
        if self.ready:
            return
        self.ready = True
        self.load.wait()
        all_in(four, self.wr.at[1], self.g)

    def finish(self, three, four):
        for i, ref in enumerate((three, four)):
            rcopy(ref, ref, self.ws.at[i], self.wr.at[i], self.g.at_sib()).wait_send()


def rms(v, eps):
    return v * lax.rsqrt(jnp.mean(v * v, axis=-1, keepdims=True) + eps)


def softplus(v):
    return jnp.maximum(v, 0.0) + jnp.log1p(jnp.exp(-jnp.abs(v)))


def silu(v):
    return v / (1.0 + jnp.exp(-v))


def front_kernel(
    n_dp, n_x,
    hidden, gain, wt, convw, convb, wlow_h, wbc_h, wdt_h, dtb, conv_h, lens, wo, ids, count,
    xs_out, z_out, filt_out, step_out, meta_out, w2_out,
    a, w, part, got, s_ref, x_ref, lb, lgot, wlow, wbc, wdt, conv, acc_low, acc_bc, w2,
    ws2, wr2, ws, wr, send, ry, r1, r2, rf, rs, ar, ls, lr, local,
):
    g = Geo(n_dp, n_x)
    ks = hidden.shape[1] // n_x
    friends = greet(g)
    cols = pl.ds(pl.multiple_of(g.x * ks, 128), ks)
    loads = [
        pltpu.make_async_copy(src, dst, local.at[i + 1])
        for i, (src, dst) in enumerate(((conv_h, conv), (wlow_h, wlow), (wbc_h, wbc), (wdt_h, wdt)))
    ]
    weights = Weights(
        g, n_x, g.x, g.at_x, lambda j: wt.at[:, :, pl.ds(pl.multiple_of(j * ks, 128), ks)],
        lambda j, c: w.at[j, :, c], (ws, wr), local.at[0],
    )
    w_three, w_four = w.at[pl.ds(0, n_x - 1), :, 0], w.at[:, :, 0]
    weights.load.start()

    sel_t = slots(ids, count)
    sel = jnp.transpose(sel_t)[:ROWS].astype(BF)
    sel_tb = sel_t[:, :ROWS].astype(BF)
    h = hidden[...].astype(F32)
    scale = lax.rsqrt(jnp.mean(h * h, axis=-1, keepdims=True) + 1e-05)
    normed = (hidden[:, cols].astype(F32) * scale * gain[:, cols]).astype(BF)
    my_rows = pl.ds(pl.multiple_of(g.y * ROWS, 8), ROWS)
    a[g.z, my_rows] = jnp.dot(sel, normed, preferred_element_type=F32).astype(BF)
    greeted(friends)

    weights.start()

    def load_all():
        for load in loads:
            load.start()

    def w2d():
        weights.wait(w_four)
        return w[...].reshape(n_x * 128, ks)

    n = ids.shape[1]
    eye = lax.broadcasted_iota(jnp.int32, (n, n), 0) == lax.broadcasted_iota(jnp.int32, (n, n), 1)
    length = jnp.sum(
        jnp.where(eye, jnp.broadcast_to(lens[...].astype(F32), (n, n)), 0.0), axis=1, keepdims=True
    )
    taps = convw.shape[0]
    usable = [jnp.where(length >= float(taps - 1 - k), 1.0, 0.0) for k in range(taps - 1)]
    lane = lax.broadcasted_iota(jnp.int32, (ROWS, 128), 1)
    span = NY * 64
    acc_low[...] = jnp.zeros_like(acc_low)
    acc_bc[...] = jnp.zeros_like(acc_bc)
    arrivals = list(FRONT_ARRIVAL)

    def consume(arrived):
        if len(arrivals) == len(FRONT_ARRIVAL):
            for load in loads:
                load.wait()
        grp = arrived(*arrivals.pop(0))
        ch = pl.ds(pl.multiple_of(grp * span, span), span)
        x_parts, z_parts = [], []
        for p in range(NY // 2):
            b0 = x_ref[grp * NY + 2 * p].astype(F32)
            b1 = x_ref[grp * NY + 2 * p + 1].astype(F32)
            x_parts.append(jnp.where(lane < 64, b0, pltpu.roll(b1, 64, 1)))
            z_parts.append(jnp.where(lane < 64, pltpu.roll(b0, 64, 1), b1))
        x_c = jnp.concatenate(x_parts, axis=1).astype(BF)
        z_c = jnp.concatenate(z_parts, axis=1).astype(BF)
        xs = jnp.dot(sel_tb, x_c, preferred_element_type=F32)
        zs = jnp.dot(sel_tb, z_c, preferred_element_type=F32)
        xs_out[:, ch] = xs.astype(BF)
        z_out[:, ch] = silu(zs)
        total = xs * convw[taps - 1 : taps, ch]
        for k in range(taps - 1):
            total = total + conv[k, :, ch].astype(F32) * (convw[k : k + 1, ch] * usable[k])
        filt = silu(total + convb[:, ch]).astype(BF)
        filt_out[:, ch] = filt.astype(F32)
        acc_low[...] += jnp.dot(filt, wlow[ch, :], preferred_element_type=F32)
        acc_bc[...] += lax.dot_general(
            filt, wbc[:, ch], (((1,), (1,)), ((), ())), preferred_element_type=F32
        )

    arrived, finish = stage(
        g, a, w2d, part, got, (s_ref, x_ref), g.x, g.at_x, n_x, (send, ry, r1, r2, rf, rs, ar),
        lambda e: a.at[g.z, my_rows], ks // 2, ks // 2, FRONT_ORDER, FRONT_PLAN, load_all,
        lambda: weights.relay(w_three), consume,
    )
    k2 = wo.shape[1] // NY
    out_weights = Weights(
        g, NY, g.y, lambda j: g.at(g.z, j), lambda j: wo.at[:, pl.ds(pl.multiple_of(j * k2, 128), k2)],
        lambda j, c: w2.at[j, c], (ws2, wr2), local.at[0],
    )
    w2_three, w2_four = w2.at[pl.ds(0, NY - 1), 0], w2.at[:, 0]
    out_weights.load.start()
    out_weights.start()
    for _ in range(len(arrivals)):
        consume(arrived)

    rank = wlow.shape[1]
    nb = wbc.shape[0]
    lb[...] = jnp.zeros_like(lb)
    lb[:, :rank] = acc_low[...].astype(BF)
    lb[:, rank : rank + nb] = acc_bc[...].astype(BF)

    for e in range(1, n_x):
        rcopy(lb, lgot.at[e - 1], ls, lr, g.at_x(lax.rem(g.x + e, n_x))).start()
    out_weights.relay(w2_three)
    acc = lb[...].astype(F32)
    all_in(lgot, lr, g)
    for e in range(1, n_x):
        acc = acc + lgot[e - 1].astype(F32)
    out_weights.wait(w2_four)
    w2_out[...] = w2[...]
    low = rms(acc[:, :rank], 1e-06).astype(BF)
    step_out[...] = softplus(jnp.dot(low, wdt[...], preferred_element_type=F32) + dtb[...])
    bc = acc[:, rank : rank + 128]
    li = lax.broadcasted_iota(jnp.int32, bc.shape, 1)
    half = nb // 2
    is_b = li < half
    is_c = jnp.logical_and(li >= half, li < nb)
    sq = bc * bc
    mb = jnp.sum(jnp.where(is_b, sq, 0.0), axis=1, keepdims=True) * (1.0 / half)
    mc = jnp.sum(jnp.where(is_c, sq, 0.0), axis=1, keepdims=True) * (1.0 / half)
    live = jnp.sum(sel_t, axis=1, keepdims=True)
    fresh = jnp.where(length > 0.0, 1.0, 0.0)
    meta = bc * jnp.where(is_b, lax.rsqrt(mb + 1e-06), lax.rsqrt(mc + 1e-06))
    meta = jnp.where(li == nb, live, meta)
    meta_out[...] = jnp.where(li == nb + 1, fresh, meta)

    rcopy(lgot, lgot, ls, lr, g.at_sib()).wait_send()
    weights.finish(w_three, w_four)
    out_weights.finish(w2_three, w2_four)
    finish()


def state_kernel(
    ids, count, xs, zg, filt, step, meta, alog, dskip, conv, state, gated, conv_next, state_next,
    rate, gated_f, conv_v, rows, sems,
):
    n_slot, n_state, width = state.shape

    def keep(k, carry):
        s = ids[0, k]
        pltpu.make_async_copy(state.at[s], state_next.at[s], sems.at[0]).start()
        return carry

    lax.fori_loop(count[0], n_slot, keep, 0)

    live = meta[:, 2 * n_state : 2 * n_state + 1] > 0.5
    window = [conv[1], conv[2], xs[...]]
    for k in range(3):
        conv_v[k] = jnp.where(live, window[k].astype(F32), conv[k].astype(F32)).astype(BF)
    conv_copy = pltpu.make_async_copy(conv_v, conv_next, sems.at[1])
    conv_copy.start()

    rate[...] = -jnp.exp(alog[...])
    row_i = lax.broadcasted_iota(jnp.int32, (n_state, 128), 0)
    lane_i = lax.broadcasted_iota(jnp.int32, (n_state, 128), 1)
    chunk = 512
    gated_f[...] = jnp.zeros_like(gated_f)

    def one(k, carry):
        s = ids[0, k]
        mrow = jnp.broadcast_to(meta[pl.ds(s, 1), :], (n_state, 128))
        b = jnp.sum(jnp.where(lane_i == row_i, mrow, 0.0), axis=1, keepdims=True)
        cc = jnp.sum(jnp.where(lane_i == row_i + n_state, mrow, 0.0), axis=1, keepdims=True)
        fresh = jnp.sum(jnp.where(lane_i == 2 * n_state + 1, mrow, 0.0), axis=1, keepdims=True)
        for t in range(width // chunk):
            sl = slice(t * chunk, (t + 1) * chunk)
            st = step[pl.ds(s, 1), sl]
            f = filt[pl.ds(s, 1), sl]
            upd = jnp.exp(rate[:, sl] * st) * (state[s, :, sl] * fresh) + b * (st * f)
            rows[s, :, sl] = upd
            y = jnp.sum(cc * upd, axis=0, keepdims=True) + dskip[:, sl] * f
            gated_f[pl.ds(s, 1), sl] = y * zg[pl.ds(s, 1), sl]
        pltpu.make_async_copy(rows.at[s], state_next.at[s], sems.at[0]).start()
        return carry

    lax.fori_loop(0, count[0], one, 0)
    gated[...] = gated_f[...].astype(BF)
    conv_copy.wait()
    pltpu.make_async_copy(rows, state_next, sems.at[0]).wait()


def back_kernel(
    n_dp, n_x,
    hidden_h, gated, w_h, ids, count,
    mixed,
    a, part, got, s_ref, x_ref, gc, px, hidden, w,
    send, ry, r1, r2, rf, rs, ar, ls, lr, local,
):
    g = Geo(n_dp, n_x)
    ks = gated.shape[1] // NY
    friends = greet(g)
    share = pl.ds(pl.multiple_of(g.x * mixed.shape[1], 128), mixed.shape[1])
    loads = (
        pltpu.make_async_copy(w_h, w, local.at[0]),
        pltpu.make_async_copy(hidden_h.at[:, share], hidden, local.at[1]),
    )
    for load in loads:
        load.start()
    cols = pl.ds(pl.multiple_of(g.y * ks, 128), ks)
    my_rows = pl.ds(pl.multiple_of(g.y * ROWS, 8), ROWS)
    sel_t = slots(ids, count)
    sel = jnp.transpose(sel_t)[:ROWS].astype(BF)
    gc[...] = jnp.dot(sel, gated[...], preferred_element_type=F32).astype(BF)
    a[g.z, my_rows] = gc[:, cols]
    greeted(friends)

    def y_src(e):
        return gc.at[:, pl.ds(pl.multiple_of(lax.rem(g.y + e, NY) * ks, 128), ks)]

    def w2d():
        return w[...].reshape(NY * 128, ks)

    def loaded():
        for load in loads:
            load.wait()

    arrived, finish = stage(
        g, a, w2d, part, got, (s_ref, x_ref), g.y, lambda j: g.at(g.z, j), NY,
        (send, ry, r1, r2, rf, rs, ar), y_src, ks, 0, BACK_ORDER, BACK_PLAN, loaded,
    )
    per = g.nm // n_x
    for one in BACK_ORDER:
        grp = arrived(*one)
        j = grp * NY // per
        e = lax.rem(j + n_x - g.x, n_x)

        @pl.when(e != 0)
        def _():
            blks = x_ref.at[pl.ds(grp * NY, NY)]
            rcopy(blks, px.at[e - 1, pl.ds(grp * NY - j * per, NY)], ls, lr, g.at_x(j)).start()

    all_in(px, lr, g)
    for k in range(per):
        total = x_ref[g.x * per + k].astype(F32)
        for e in range(1, n_x):
            total = total + px[e - 1, k].astype(F32)
        spread = lax.dot_general(
            sel_t[:, :ROWS], total, (((1,), (0,)), ((), ())),
            precision=lax.Precision.HIGHEST, preferred_element_type=F32,
        )
        base = hidden[:, k * 128 : (k + 1) * 128].astype(F32)
        mixed[:, k * 128 : (k + 1) * 128] = (base + spread).astype(BF)

    rcopy(px, px, ls, lr, g.at_sib()).wait_send()
    finish()


def stage_scratch(nz, n_peer, ks):
    nm = nz * NY
    blk = NY * ROWS
    return [
        pltpu.VMEM((n_peer, nz, blk, 128), BF),
        pltpu.VMEM((n_peer - 1, nz, blk, 128), BF),
        pltpu.VMEM((nz, blk, 128), BF),
        pltpu.VMEM((nm, ROWS, 128), BF),
    ]


def stage_sems(nz):
    dma = pltpu.SemaphoreType.DMA
    far = nz // 2
    return [
        dma((5,)), dma, dma((2, far, NY)), dma((2, far)), dma((nz - 1,)), dma((nz,)),
        dma((nz,)), dma, dma,
    ]


def in_hbm(v):
    return pltpu.with_memory_space_constraint(v, pltpu.HBM)


def body(
    n_dp, n_x,
    hidden_in, norm_gain, w_in, conv_w, conv_b, w_dt_low, w_bc, w_dt, dt_bias, a_log, d_skip, w_out,
    conv_state, ssm_state, lengths, active_ids, active_count,
):
    n_slot, depth = hidden_in.shape
    width = conv_w.shape[1]
    nz = n_dp // (NY * NC)
    ka = depth // n_x
    kc = width // NY
    vm = pl.BlockSpec(memory_space=pltpu.VMEM)
    sm = pl.BlockSpec(memory_space=pltpu.SMEM)
    hbm = pl.BlockSpec(memory_space=pltpu.HBM)
    wt = jnp.transpose(w_in, (1, 2, 3, 0)).reshape(2, w_in.shape[3], depth)
    wo = jnp.transpose(w_out)
    conv_t = jnp.transpose(conv_state, (1, 0, 2))
    sds = jax.ShapeDtypeStruct
    blk = NY * ROWS

    xs, zg, filt, step, meta, w2 = pl.pallas_call(
        functools.partial(front_kernel, n_dp, n_x),
        name="front",
        out_shape=(
            sds((n_slot, width), BF), sds((n_slot, width), F32), sds((n_slot, width), F32),
            sds((n_slot, width), F32), sds((n_slot, 128), F32), sds((NY, NC, wo.shape[0], kc), BF),
        ),
        in_specs=[vm, vm, hbm, vm, vm, hbm, hbm, hbm, vm, hbm, vm, hbm, vm, sm],
        out_specs=(vm,) * 6,
        scratch_shapes=[
            pltpu.VMEM((nz, blk, ka), BF),
            pltpu.VMEM((n_x, 2, NC, w_in.shape[3], ka), BF),
            *stage_scratch(nz, n_x, ka),
            pltpu.VMEM((n_slot, w_dt_low.shape[1] + 128), BF),
            pltpu.VMEM((n_x - 1, n_slot, w_dt_low.shape[1] + 128), BF),
            pltpu.VMEM(w_dt_low.shape, BF),
            pltpu.VMEM(w_bc.shape, BF),
            pltpu.VMEM(w_dt.shape, BF),
            pltpu.VMEM(conv_t.shape, BF),
            pltpu.VMEM((n_slot, w_dt_low.shape[1]), F32),
            pltpu.VMEM((n_slot, w_bc.shape[0]), F32),
            pltpu.VMEM((NY, NC, wo.shape[0], kc), BF),
            *[pltpu.SemaphoreType.DMA((2,))] * 4,
            *stage_sems(nz),
            pltpu.SemaphoreType.DMA((5,)),
        ],
        compiler_params=pltpu.CompilerParams(collective_id=0, has_side_effects=True, vmem_limit_bytes=18 << 20),
        cost_estimate=pl.CostEstimate(flops=20_000_000_000, bytes_accessed=4_000_000, transcendentals=0),
    )(
        *map(
            in_hbm,
            (
                hidden_in, norm_gain.reshape(1, depth), wt, conv_w, conv_b.reshape(1, width), w_dt_low, w_bc, w_dt,
                dt_bias.reshape(1, width), conv_t, lengths.reshape(1, n_slot), wo, active_ids,
            ),
        ),
        active_count,
    )

    n_state = a_log.shape[0]
    gated, conv_next, ssm_next = pl.pallas_call(
        state_kernel,
        name="state",
        out_shape=(
            sds((n_slot, width), BF), sds((3, n_slot, width), BF), sds(ssm_state.shape, F32),
        ),
        in_specs=[sm, sm] + [vm] * 9,
        out_specs=(vm, hbm, hbm),
        scratch_shapes=[
            pltpu.VMEM((n_state, width), F32), pltpu.VMEM((n_slot, width), F32),
            pltpu.VMEM((3, n_slot, width), BF), pltpu.VMEM(ssm_state.shape, F32), pltpu.SemaphoreType.DMA((2,)),
        ],
        compiler_params=pltpu.CompilerParams(vmem_limit_bytes=20 << 20),
        cost_estimate=pl.CostEstimate(flops=20_000_000, bytes_accessed=8_000_000, transcendentals=800_000),
    )(active_ids, active_count, xs, zg, filt, step, meta, a_log, d_skip.reshape(1, width), conv_t, ssm_state)

    mixed = pl.pallas_call(
        functools.partial(back_kernel, n_dp, n_x),
        name="back",
        out_shape=sds((n_slot, depth // n_x), BF),
        in_specs=[hbm, vm, hbm, vm, sm],
        out_specs=vm,
        scratch_shapes=[
            pltpu.VMEM((nz, blk, kc), BF),
            *stage_scratch(nz, NY, kc),
            pltpu.VMEM((ROWS, width), BF),
            pltpu.VMEM((n_x - 1, nz * NY // n_x, ROWS, 128), BF),
            pltpu.VMEM((n_slot, depth // n_x), BF),
            pltpu.VMEM(w2.shape, BF),
            *stage_sems(nz),
            pltpu.SemaphoreType.DMA((2,)),
        ],
        compiler_params=pltpu.CompilerParams(collective_id=1, has_side_effects=True, vmem_limit_bytes=18 << 20),
        cost_estimate=pl.CostEstimate(flops=20_000_000_000, bytes_accessed=4_000_000, transcendentals=0),
    )(hidden_in, gated, w2, active_ids, active_count)
    return (mixed, jnp.transpose(conv_next, (1, 0, 2)), ssm_next)


def solution(mesh):
    in_specs = (
        P("dp", None),
        P(),
        P(None, None, "tensor", "dp"),
        P(None, "tensor"),
        P("tensor"),
        P("tensor", None),
        P(None, "tensor"),
        P(None, "tensor"),
        P("tensor"),
        P(None, "tensor"),
        P("tensor"),
        P("tensor", "dp"),
        P("dp", None, "tensor"),
        P("dp", None, "tensor"),
        P("dp"),
        P("dp", None),
        P("dp"),
    )
    out_specs = (P("dp", "tensor"), P("dp", None, "tensor"), P("dp", None, "tensor"))
    run = functools.partial(body, mesh.shape["dp"], mesh.shape["tensor"])
    return jax.shard_map(run, mesh=mesh, in_specs=in_specs, out_specs=out_specs, check_vma=False)
```

```python
import functools

import jax
import jax.numpy as jnp
from jax import lax
from jax.experimental import pallas as pl
from jax.experimental.pallas import tpu as pltpu
from jax.sharding import PartitionSpec as P

MESH = pl.DeviceIdType.MESH
BF = jnp.bfloat16
F32 = jnp.float32
NY, NC = 4, 2
ROWS = 24
FRONT_ORDER = ((2, 0), (2, 1), (3, 0), (3, 1), (4, 0), (1, 0), (1, 1), (0, 0))
FRONT_PLAN = ("", "r", "mmtmm", "mdmdmdmddddd")
FRONT_ARRIVAL = ((2, 0), (2, 1), (3, 0), (3, 1), (1, 0), (1, 1), (0, 0), (4, 0))
BACK_ORDER = ((0, 0), (1, 0), (1, 1), (2, 0), (2, 1), (3, 0), (3, 1), (4, 0))
BACK_PLAN = ("mmm", "mmd", "mmdddd", "mddd")


class Geo:
    def __init__(self, n_dp, n_x):
        self.nz = n_dp // (NY * NC)
        self.nm = self.nz * NY
        self.nx = n_x
        dp = lax.axis_index("dp")
        self.x = lax.axis_index("tensor")
        self.c = lax.rem(dp, NC)
        self.m = dp // NC
        self.y = lax.rem(self.m, NY)
        self.z = self.m // NY
        self.sib = NC - 1 - self.c

    def at(self, z, y):
        return ((z * NY + y) * NC + self.c, self.x)

    def at_m(self, m):
        return (m * NC + self.c, self.x)

    def at_x(self, x):
        return (self.m * NC + self.c, x)

    def at_sib(self):
        return (self.m * NC + self.sib, self.x)


def rcopy(src, dst, send, recv, dev):
    return pltpu.make_async_remote_copy(
        src_ref=src, dst_ref=dst, send_sem=send, recv_sem=recv, device_id=dev, device_id_type=MESH
    )


def greet(g):
    sem = pltpu.get_barrier_semaphore()
    devs = [g.at(lax.rem(g.z + dz, g.nz), lax.rem(g.y + e, NY)) for dz in (1, g.nz - 1) for e in range(NY)]
    devs += [g.at(g.z, lax.rem(g.y + e, NY)) for e in range(1, NY)]
    devs += [g.at_x(lax.rem(g.x + e, g.nx)) for e in range(1, g.nx)]
    devs.append(g.at_sib())
    for dev in devs:
        pl.semaphore_signal(sem, inc=1, device_id=dev, device_id_type=MESH)
    return len(devs)


def greeted(count):
    pl.semaphore_wait(pltpu.get_barrier_semaphore(), count)


def slots(ids_ref, count_ref):
    n = ids_ref.shape[1]
    slot = lax.broadcasted_iota(jnp.int32, (n, n), 0)
    order = lax.broadcasted_iota(jnp.int32, (n, n), 1)
    live = jnp.logical_and(order < count_ref[0], order < ROWS)
    hit = jnp.logical_and(slot == jnp.broadcast_to(ids_ref[...], (n, n)), live)
    sel = jnp.where(hit, 1.0, 0.0).astype(F32)
    return sel


def all_in(ref, sem, g):
    rcopy(ref, ref, sem, sem, g.at_sib()).wait_recv()


def stage(g, a, w2d, part, got, summed, own, peer, n_peer, sems, y_src, k1, k2, muls, plan, after_start, relay=None, consume=None):
    send, ry, r1, r2, rf, rs, ar = sems
    s_ref, x_ref = summed
    nz = g.nz
    far = nz // 2
    half = NY // 2
    first = jnp.where(lax.rem(g.z, far) >= far // 2, 0, 1)
    dirs = (first, 1 - first)

    def rows(q):
        return pl.ds(pl.multiple_of(q * ROWS, 8), ROWS)

    def blk(grp, d):
        return a.at[grp, rows(lax.rem(g.y + d, NY)), pl.ds(0, k1)]

    def blk2(grp, d):
        return a.at[grp, rows(lax.rem(g.y + d, NY)), pl.ds(k1, k2)]

    def group(s, q):
        if s == 0:
            return g.z, 0
        return lax.rem(g.z + nz + (2 * q - 1) * s, nz), (s + q * far if s < far else far)

    def seen_by(s, q):
        if s == 0 or s == far:
            return s
        return s + (1 - q) * far

    def next_z(q):
        return lax.rem(g.z + nz + 1 - 2 * q, nz)

    def ring(s, q, i, grp):
        d = lax.rem(half * q + i, NY)
        return rcopy(blk(grp, d), blk(grp, d), send.at[0], r1.at[q, s - 1, d], g.at(next_z(q), g.y))

    def ring2(s, q, grp):
        return rcopy(blk2(grp, 0), blk2(grp, 0), send.at[1], r2.at[q, s - 1], g.at(next_z(q), g.y))

    def fan(grp, gi, e):
        dev = g.at(g.z, lax.rem(g.y + e, NY))
        return rcopy(blk2(grp, 0), blk2(grp, 0), send.at[1], rf.at[gi - 1], dev)

    def multiply(s, q):
        grp, gi = group(s, q)
        if s == 0:
            all_in(a.at[g.z, pl.ds(0, (NY - 1) * ROWS)], ry, g)
        elif k2:
            all_in(a.at[grp, pl.ds(0, (NY - 1) * ROWS), pl.ds(k1, k2)], rf.at[gi - 1], g)
        res = lax.dot_general(a[grp], w2d(), (((1,), (1,)), ((), ())), preferred_element_type=F32)
        for j in range(n_peer):
            part[j, grp] = res[:, j * 128 : (j + 1) * 128].astype(BF)
        for e in range(1, n_peer):
            j = lax.rem(own + e, n_peer)
            rcopy(part.at[j, grp], got.at[e - 1, grp], send.at[2], rs.at[gi], peer(j)).start()

    def drain(s, q):
        grp, gi = group(s, q)
        all_in(got.at[:, grp], rs.at[gi], g)
        total = part[own, grp].astype(F32)
        for e in range(1, n_peer):
            total = total + got[e - 1, grp].astype(F32)
        s_ref[grp] = total.astype(BF)
        for d in range(NY):
            y = lax.rem(g.y + d, NY)
            if s == 0 and d == 0:
                x_ref[g.m] = s_ref[grp, rows(y)]
            else:
                sem = ar.at[seen_by(s, q)]
                rcopy(s_ref.at[grp, rows(y)], x_ref.at[g.m], send.at[3], sem, g.at(grp, y)).start()

    mine = rows(g.y)
    for q in dirs:
        if k2:
            ring2(1, q, g.z).start()
    for e in range(NY):
        for q in dirs:
            src = y_src(e)
            dst = a.at[g.z, mine, pl.ds(0, k1)]
            dev = g.at(next_z(q), lax.rem(g.y + e, NY))
            rcopy(src.at[:, pl.ds(0, k1)], dst, send.at[0], r1.at[q, 0, (NY - e) % NY], dev).start()
    for e in range(1, NY):
        rcopy(y_src(e), a.at[g.z, mine], send.at[4], ry, g.at(g.z, lax.rem(g.y + e, NY))).start()
    after_start()

    def arrived(s, i):
        q = dirs[i] if s < far else 0
        grp, gi = group(s, q)
        n = NY if s else NY - 1
        all_in(x_ref.at[pl.ds(grp * NY, n)], ar.at[gi], g)
        return grp

    to_multiply = [(s, dirs[i] if s < far else 0) for s, i in muls]
    to_drain = list(to_multiply)

    def turn(s):
        for q in dirs if s < far else (0,):
            grp, gi = group(s, q)
            ring2(s, q, grp).wait_recv()
            if s + 1 < far:
                ring2(s + 1, q, grp).start()
            elif s < far:

                @pl.when(q == 0)
                def _():
                    ring2(far, 0, grp).start()

            for e in range(1, NY):
                fan(grp, gi, e).start()

    for s in range(1, far + 1):
        if k2 and s < far:
            turn(s)
        for i in range(NY if s < far else half):
            for q in dirs:
                grp, gi = group(s, q)
                ring(s, q, i, grp).wait_recv()
                if s + 1 < far or (s < far and i < half):
                    ring(s + 1, q, i, grp).start()
        for what in plan[s - 1]:
            if what == "m":
                multiply(*to_multiply.pop(0))
            elif what == "d":
                drain(*to_drain.pop(0))
            elif what == "r":
                relay()
            elif what == "c":
                consume(arrived)
            else:
                turn(far)

    def finish():
        def sent(ref, i):
            rcopy(ref, ref, send.at[i], ry, g.at_sib()).wait_send()

        sent(a.at[pl.ds(0, nz - 1), :, pl.ds(0, k1)], 0)
        if k2:
            sent(a.at[pl.ds(0, nz - 1), :, pl.ds(k1, k2)], 1)
        sent(got, 2)
        sent(x_ref.at[pl.ds(0, g.nm - 1)], 3)
        sent(a.at[0, pl.ds(0, (NY - 1) * ROWS)], 4)

    return arrived, finish


class Weights:
    def __init__(self, g, n, me, dev, src, dst, sems, local):
        self.g, self.n, self.me, self.dev, self.src, self.dst = g, n, me, dev, src, dst
        self.ws, self.wr = sems
        self.load = pltpu.make_async_copy(src(me), dst(me, g.c), local)
        self.ready = False

    def start(self):
        for e in range(1, self.n):
            j = lax.rem(self.me + e, self.n)
            rcopy(self.src(j), self.dst(self.me, self.g.c), self.ws.at[0], self.wr.at[0], self.dev(j)).start()
        own = self.dst(self.me, self.g.c)
        rcopy(self.src(self.me), own, self.ws.at[1], self.wr.at[1], self.g.at_sib()).start()

    def relay(self, three):
        all_in(three, self.wr.at[0], self.g)
        for e in range(1, self.n):
            blk = self.dst(lax.rem(self.me + e, self.n), self.g.c)
            rcopy(blk, blk, self.ws.at[1], self.wr.at[1], self.g.at_sib()).start()

    def wait(self, four):
        if self.ready:
            return
        self.ready = True
        self.load.wait()
        all_in(four, self.wr.at[1], self.g)

    def finish(self, three, four):
        for i, ref in enumerate((three, four)):
            rcopy(ref, ref, self.ws.at[i], self.wr.at[i], self.g.at_sib()).wait_send()


def rms(v, eps):
    return v * lax.rsqrt(jnp.mean(v * v, axis=-1, keepdims=True) + eps)


def softplus(v):
    return jnp.maximum(v, 0.0) + jnp.log1p(jnp.exp(-jnp.abs(v)))


def silu(v):
    return v / (1.0 + jnp.exp(-v))


def front_kernel(
    n_dp, n_x,
    hidden, gain, wt, convw, convb, wlow_h, wbc_h, wdt_h, dtb, conv_h, lens, wo, ids, count,
    xs_out, z_out, filt_out, step_out, meta_out, w2_out,
    a, w, part, got, s_ref, x_ref, lb, lgot, wlow, wbc, wdt, conv, acc_low, acc_bc, w2,
    ws2, wr2, ws, wr, send, ry, r1, r2, rf, rs, ar, ls, lr, local,
):
    g = Geo(n_dp, n_x)
    ks = hidden.shape[1] // n_x
    friends = greet(g)
    cols = pl.ds(pl.multiple_of(g.x * ks, 128), ks)
    loads = [
        pltpu.make_async_copy(src, dst, local.at[i + 1])
        for i, (src, dst) in enumerate(((conv_h, conv), (wlow_h, wlow), (wbc_h, wbc), (wdt_h, wdt)))
    ]
    weights = Weights(
        g, n_x, g.x, g.at_x, lambda j: wt.at[:, :, pl.ds(pl.multiple_of(j * ks, 128), ks)],
        lambda j, c: w.at[j, :, c], (ws, wr), local.at[0],
    )
    w_three, w_four = w.at[pl.ds(0, n_x - 1), :, 0], w.at[:, :, 0]
    weights.load.start()

    sel_t = slots(ids, count)
    sel = jnp.transpose(sel_t)[:ROWS].astype(BF)
    sel_tb = sel_t[:, :ROWS].astype(BF)
    h = hidden[...].astype(F32)
    scale = lax.rsqrt(jnp.mean(h * h, axis=-1, keepdims=True) + 1e-05)
    normed = (hidden[:, cols].astype(F32) * scale * gain[:, cols]).astype(BF)
    my_rows = pl.ds(pl.multiple_of(g.y * ROWS, 8), ROWS)
    a[g.z, my_rows] = jnp.dot(sel, normed, preferred_element_type=F32).astype(BF)
    greeted(friends)

    weights.start()

    def load_all():
        for load in loads:
            load.start()

    def w2d():
        weights.wait(w_four)
        return w[...].reshape(n_x * 128, ks)

    n = ids.shape[1]
    eye = lax.broadcasted_iota(jnp.int32, (n, n), 0) == lax.broadcasted_iota(jnp.int32, (n, n), 1)
    length = jnp.sum(
        jnp.where(eye, jnp.broadcast_to(lens[...].astype(F32), (n, n)), 0.0), axis=1, keepdims=True
    )
    taps = convw.shape[0]
    usable = [jnp.where(length >= float(taps - 1 - k), 1.0, 0.0) for k in range(taps - 1)]
    lane = lax.broadcasted_iota(jnp.int32, (ROWS, 128), 1)
    span = NY * 64
    acc_low[...] = jnp.zeros_like(acc_low)
    acc_bc[...] = jnp.zeros_like(acc_bc)
    arrivals = list(FRONT_ARRIVAL)

    def consume(arrived):
        if len(arrivals) == len(FRONT_ARRIVAL):
            for load in loads:
                load.wait()
        grp = arrived(*arrivals.pop(0))
        ch = pl.ds(pl.multiple_of(grp * span, span), span)
        x_parts, z_parts = [], []
        for p in range(NY // 2):
            b0 = x_ref[grp * NY + 2 * p].astype(F32)
            b1 = x_ref[grp * NY + 2 * p + 1].astype(F32)
            x_parts.append(jnp.where(lane < 64, b0, pltpu.roll(b1, 64, 1)))
            z_parts.append(jnp.where(lane < 64, pltpu.roll(b0, 64, 1), b1))
        x_c = jnp.concatenate(x_parts, axis=1).astype(BF)
        z_c = jnp.concatenate(z_parts, axis=1).astype(BF)
        xs = jnp.dot(sel_tb, x_c, preferred_element_type=F32)
        zs = jnp.dot(sel_tb, z_c, preferred_element_type=F32)
        xs_out[:, ch] = xs.astype(BF)
        z_out[:, ch] = silu(zs)
        total = xs * convw[taps - 1 : taps, ch]
        for k in range(taps - 1):
            total = total + conv[k, :, ch].astype(F32) * (convw[k : k + 1, ch] * usable[k])
        filt = silu(total + convb[:, ch]).astype(BF)
        filt_out[:, ch] = filt.astype(F32)
        acc_low[...] += jnp.dot(filt, wlow[ch, :], preferred_element_type=F32)
        acc_bc[...] += lax.dot_general(
            filt, wbc[:, ch], (((1,), (1,)), ((), ())), preferred_element_type=F32
        )

    arrived, finish = stage(
        g, a, w2d, part, got, (s_ref, x_ref), g.x, g.at_x, n_x, (send, ry, r1, r2, rf, rs, ar),
        lambda e: a.at[g.z, my_rows], ks // 2, ks // 2, FRONT_ORDER, FRONT_PLAN, load_all,
        lambda: weights.relay(w_three), consume,
    )
    k2 = wo.shape[1] // NY
    out_weights = Weights(
        g, NY, g.y, lambda j: g.at(g.z, j), lambda j: wo.at[:, pl.ds(pl.multiple_of(j * k2, 128), k2)],
        lambda j, c: w2.at[j, c], (ws2, wr2), local.at[0],
    )
    w2_three, w2_four = w2.at[pl.ds(0, NY - 1), 0], w2.at[:, 0]
    out_weights.load.start()
    out_weights.start()
    for _ in range(len(arrivals)):
        consume(arrived)

    rank = wlow.shape[1]
    nb = wbc.shape[0]
    lb[...] = jnp.zeros_like(lb)
    lb[:, :rank] = acc_low[...].astype(BF)
    lb[:, rank : rank + nb] = acc_bc[...].astype(BF)

    for e in range(1, n_x):
        rcopy(lb, lgot.at[e - 1], ls, lr, g.at_x(lax.rem(g.x + e, n_x))).start()
    out_weights.relay(w2_three)
    acc = lb[...].astype(F32)
    all_in(lgot, lr, g)
    for e in range(1, n_x):
        acc = acc + lgot[e - 1].astype(F32)
    out_weights.wait(w2_four)
    w2_out[...] = w2[...]
    low = rms(acc[:, :rank], 1e-06).astype(BF)
    step_out[...] = softplus(jnp.dot(low, wdt[...], preferred_element_type=F32) + dtb[...])
    bc = acc[:, rank : rank + 128]
    li = lax.broadcasted_iota(jnp.int32, bc.shape, 1)
    half = nb // 2
    is_b = li < half
    is_c = jnp.logical_and(li >= half, li < nb)
    sq = bc * bc
    mb = jnp.sum(jnp.where(is_b, sq, 0.0), axis=1, keepdims=True) * (1.0 / half)
    mc = jnp.sum(jnp.where(is_c, sq, 0.0), axis=1, keepdims=True) * (1.0 / half)
    live = jnp.sum(sel_t, axis=1, keepdims=True)
    fresh = jnp.where(length > 0.0, 1.0, 0.0)
    meta = bc * jnp.where(is_b, lax.rsqrt(mb + 1e-06), lax.rsqrt(mc + 1e-06))
    meta = jnp.where(li == nb, live, meta)
    meta_out[...] = jnp.where(li == nb + 1, fresh, meta)

    rcopy(lgot, lgot, ls, lr, g.at_sib()).wait_send()
    weights.finish(w_three, w_four)
    out_weights.finish(w2_three, w2_four)
    finish()


def state_kernel(
    ids, count, xs, zg, filt, step, meta, alog, dskip, conv, state, gated, conv_next, state_next,
    rate, gated_f, conv_v, rows, sems,
):
    n_slot, n_state, width = state.shape

    def keep(k, carry):
        s = ids[0, k]
        pltpu.make_async_copy(state.at[s], state_next.at[s], sems.at[0]).start()
        return carry

    lax.fori_loop(count[0], n_slot, keep, 0)

    live = meta[:, 2 * n_state : 2 * n_state + 1] > 0.5
    window = [conv[1], conv[2], xs[...]]
    for k in range(3):
        conv_v[k] = jnp.where(live, window[k].astype(F32), conv[k].astype(F32)).astype(BF)
    conv_copy = pltpu.make_async_copy(conv_v, conv_next, sems.at[1])
    conv_copy.start()

    rate[...] = -jnp.exp(alog[...])
    row_i = lax.broadcasted_iota(jnp.int32, (n_state, 128), 0)
    lane_i = lax.broadcasted_iota(jnp.int32, (n_state, 128), 1)
    chunk = 512
    gated_f[...] = jnp.zeros_like(gated_f)

    def one(k, carry):
        s = ids[0, k]
        mrow = jnp.broadcast_to(meta[pl.ds(s, 1), :], (n_state, 128))
        b = jnp.sum(jnp.where(lane_i == row_i, mrow, 0.0), axis=1, keepdims=True)
        cc = jnp.sum(jnp.where(lane_i == row_i + n_state, mrow, 0.0), axis=1, keepdims=True)
        fresh = jnp.sum(jnp.where(lane_i == 2 * n_state + 1, mrow, 0.0), axis=1, keepdims=True)
        for t in range(width // chunk):
            sl = slice(t * chunk, (t + 1) * chunk)
            st = step[pl.ds(s, 1), sl]
            f = filt[pl.ds(s, 1), sl]
            upd = jnp.exp(rate[:, sl] * st) * (state[s, :, sl] * fresh) + b * (st * f)
            rows[s, :, sl] = upd
            y = jnp.sum(cc * upd, axis=0, keepdims=True) + dskip[:, sl] * f
            gated_f[pl.ds(s, 1), sl] = y * zg[pl.ds(s, 1), sl]
        pltpu.make_async_copy(rows.at[s], state_next.at[s], sems.at[0]).start()
        return carry

    lax.fori_loop(0, count[0], one, 0)
    gated[...] = gated_f[...].astype(BF)
    conv_copy.wait()
    pltpu.make_async_copy(rows, state_next, sems.at[0]).wait()


def back_kernel(
    n_dp, n_x,
    hidden_h, gated, w_h, ids, count,
    mixed,
    a, part, got, s_ref, x_ref, gc, px, hidden, w,
    send, ry, r1, r2, rf, rs, ar, ls, lr, local,
):
    g = Geo(n_dp, n_x)
    ks = gated.shape[1] // NY
    friends = greet(g)
    share = pl.ds(pl.multiple_of(g.x * mixed.shape[1], 128), mixed.shape[1])
    loads = (
        pltpu.make_async_copy(w_h, w, local.at[0]),
        pltpu.make_async_copy(hidden_h.at[:, share], hidden, local.at[1]),
    )
    for load in loads:
        load.start()
    cols = pl.ds(pl.multiple_of(g.y * ks, 128), ks)
    my_rows = pl.ds(pl.multiple_of(g.y * ROWS, 8), ROWS)
    sel_t = slots(ids, count)
    sel = jnp.transpose(sel_t)[:ROWS].astype(BF)
    gc[...] = jnp.dot(sel, gated[...], preferred_element_type=F32).astype(BF)
    a[g.z, my_rows] = gc[:, cols]
    greeted(friends)

    def y_src(e):
        return gc.at[:, pl.ds(pl.multiple_of(lax.rem(g.y + e, NY) * ks, 128), ks)]

    def w2d():
        return w[...].reshape(NY * 128, ks)

    def loaded():
        for load in loads:
            load.wait()

    arrived, finish = stage(
        g, a, w2d, part, got, (s_ref, x_ref), g.y, lambda j: g.at(g.z, j), NY,
        (send, ry, r1, r2, rf, rs, ar), y_src, ks, 0, BACK_ORDER, BACK_PLAN, loaded,
    )
    per = g.nm // n_x
    for one in BACK_ORDER:
        grp = arrived(*one)
        j = grp * NY // per
        e = lax.rem(j + n_x - g.x, n_x)

        @pl.when(e != 0)
        def _():
            blks = x_ref.at[pl.ds(grp * NY, NY)]
            rcopy(blks, px.at[e - 1, pl.ds(grp * NY - j * per, NY)], ls, lr, g.at_x(j)).start()

    all_in(px, lr, g)
    for k in range(per):
        total = x_ref[g.x * per + k].astype(F32)
        for e in range(1, n_x):
            total = total + px[e - 1, k].astype(F32)
        spread = lax.dot_general(
            sel_t[:, :ROWS], total, (((1,), (0,)), ((), ())),
            precision=lax.Precision.HIGHEST, preferred_element_type=F32,
        )
        base = hidden[:, k * 128 : (k + 1) * 128].astype(F32)
        mixed[:, k * 128 : (k + 1) * 128] = (base + spread).astype(BF)

    rcopy(px, px, ls, lr, g.at_sib()).wait_send()
    finish()


def stage_scratch(nz, n_peer, ks):
    nm = nz * NY
    blk = NY * ROWS
    return [
        pltpu.VMEM((n_peer, nz, blk, 128), BF),
        pltpu.VMEM((n_peer - 1, nz, blk, 128), BF),
        pltpu.VMEM((nz, blk, 128), BF),
        pltpu.VMEM((nm, ROWS, 128), BF),
    ]


def stage_sems(nz):
    dma = pltpu.SemaphoreType.DMA
    far = nz // 2
    return [
        dma((5,)), dma, dma((2, far, NY)), dma((2, far)), dma((nz - 1,)), dma((nz,)),
        dma((nz,)), dma, dma,
    ]


def in_hbm(v):
    return pltpu.with_memory_space_constraint(v, pltpu.HBM)


def body(
    n_dp, n_x,
    hidden_in, norm_gain, w_in, conv_w, conv_b, w_dt_low, w_bc, w_dt, dt_bias, a_log, d_skip, w_out,
    conv_state, ssm_state, lengths, active_ids, active_count,
):
    n_slot, depth = hidden_in.shape
    width = conv_w.shape[1]
    nz = n_dp // (NY * NC)
    ka = depth // n_x
    kc = width // NY
    vm = pl.BlockSpec(memory_space=pltpu.VMEM)
    sm = pl.BlockSpec(memory_space=pltpu.SMEM)
    hbm = pl.BlockSpec(memory_space=pltpu.HBM)
    wt = jnp.transpose(w_in, (1, 2, 3, 0)).reshape(2, w_in.shape[3], depth)
    wo = jnp.transpose(w_out)
    conv_t = jnp.transpose(conv_state, (1, 0, 2))
    sds = jax.ShapeDtypeStruct
    blk = NY * ROWS

    xs, zg, filt, step, meta, w2 = pl.pallas_call(
        functools.partial(front_kernel, n_dp, n_x),
        name="front",
        out_shape=(
            sds((n_slot, width), BF), sds((n_slot, width), F32), sds((n_slot, width), F32),
            sds((n_slot, width), F32), sds((n_slot, 128), F32), sds((NY, NC, wo.shape[0], kc), BF),
        ),
        in_specs=[vm, vm, hbm, vm, vm, hbm, hbm, hbm, vm, hbm, vm, hbm, vm, sm],
        out_specs=(vm,) * 6,
        scratch_shapes=[
            pltpu.VMEM((nz, blk, ka), BF),
            pltpu.VMEM((n_x, 2, NC, w_in.shape[3], ka), BF),
            *stage_scratch(nz, n_x, ka),
            pltpu.VMEM((n_slot, w_dt_low.shape[1] + 128), BF),
            pltpu.VMEM((n_x - 1, n_slot, w_dt_low.shape[1] + 128), BF),
            pltpu.VMEM(w_dt_low.shape, BF),
            pltpu.VMEM(w_bc.shape, BF),
            pltpu.VMEM(w_dt.shape, BF),
            pltpu.VMEM(conv_t.shape, BF),
            pltpu.VMEM((n_slot, w_dt_low.shape[1]), F32),
            pltpu.VMEM((n_slot, w_bc.shape[0]), F32),
            pltpu.VMEM((NY, NC, wo.shape[0], kc), BF),
            *[pltpu.SemaphoreType.DMA((2,))] * 4,
            *stage_sems(nz),
            pltpu.SemaphoreType.DMA((5,)),
        ],
        compiler_params=pltpu.CompilerParams(collective_id=0, has_side_effects=True, vmem_limit_bytes=18 << 20),
        cost_estimate=pl.CostEstimate(flops=20_000_000_000, bytes_accessed=4_000_000, transcendentals=0),
    )(
        *map(
            in_hbm,
            (
                hidden_in, norm_gain.reshape(1, depth), wt, conv_w, conv_b.reshape(1, width), w_dt_low, w_bc, w_dt,
                dt_bias.reshape(1, width), conv_t, lengths.reshape(1, n_slot), wo, active_ids,
            ),
        ),
        active_count,
    )

    n_state = a_log.shape[0]
    gated, conv_next, ssm_next = pl.pallas_call(
        state_kernel,
        name="state",
        out_shape=(
            sds((n_slot, width), BF), sds((3, n_slot, width), BF), sds(ssm_state.shape, F32),
        ),
        in_specs=[sm, sm] + [vm] * 9,
        out_specs=(vm, hbm, hbm),
        scratch_shapes=[
            pltpu.VMEM((n_state, width), F32), pltpu.VMEM((n_slot, width), F32),
            pltpu.VMEM((3, n_slot, width), BF), pltpu.VMEM(ssm_state.shape, F32), pltpu.SemaphoreType.DMA((2,)),
        ],
        compiler_params=pltpu.CompilerParams(vmem_limit_bytes=20 << 20),
        cost_estimate=pl.CostEstimate(flops=20_000_000, bytes_accessed=8_000_000, transcendentals=800_000),
    )(active_ids, active_count, xs, zg, filt, step, meta, a_log, d_skip.reshape(1, width), conv_t, ssm_state)

    mixed = pl.pallas_call(
        functools.partial(back_kernel, n_dp, n_x),
        name="back",
        out_shape=sds((n_slot, depth // n_x), BF),
        in_specs=[hbm, vm, hbm, vm, sm],
        out_specs=vm,
        scratch_shapes=[
            pltpu.VMEM((nz, blk, kc), BF),
            *stage_scratch(nz, NY, kc),
            pltpu.VMEM((ROWS, width), BF),
            pltpu.VMEM((n_x - 1, nz * NY // n_x, ROWS, 128), BF),
            pltpu.VMEM((n_slot, depth // n_x), BF),
            pltpu.VMEM(w2.shape, BF),
            *stage_sems(nz),
            pltpu.SemaphoreType.DMA((2,)),
        ],
        compiler_params=pltpu.CompilerParams(collective_id=1, has_side_effects=True, vmem_limit_bytes=18 << 20),
        cost_estimate=pl.CostEstimate(flops=20_000_000_000, bytes_accessed=4_000_000, transcendentals=0),
    )(hidden_in, gated, w2, active_ids, active_count)
    return (mixed, jnp.transpose(conv_next, (1, 0, 2)), ssm_next)


def solution(mesh):
    in_specs = (
        P("dp", None),
        P(),
        P(None, None, "tensor", "dp"),
        P(None, "tensor"),
        P("tensor"),
        P("tensor", None),
        P(None, "tensor"),
        P(None, "tensor"),
        P("tensor"),
        P(None, "tensor"),
        P("tensor"),
        P("tensor", "dp"),
        P("dp", None, "tensor"),
        P("dp", None, "tensor"),
        P("dp"),
        P("dp", None),
        P("dp"),
    )
    out_specs = (P("dp", "tensor"), P("dp", None, "tensor"), P("dp", None, "tensor"))
    run = functools.partial(body, mesh.shape["dp"], mesh.shape["tensor"])
    return jax.shard_map(run, mesh=mesh, in_specs=in_specs, out_specs=out_specs, check_vma=False)
```
